32 devices in a mesh: grp: 2 (over x), facet: 16 (over z, y, core).
Axes of the slice: x: 2, y: 2, z: 4, core: 2. Of those that a mesh axis runs over, the one named last changes fastest.
Arguments:
- image: float32 [16, 256, 256], P(None, 'facet', 'grp'), may hold values from 0 to 2
- wavelet_dual: bfloat16 [8, 16, 256, 256], P(None, None, 'facet', 'grp'), may hold values from -6 to 6
- thresholds: float32 [8, 256, 256], P(None, 'facet', 'grp'), may hold values from 1 to 10
- filter_taps: float32 [8, 2, 7], replicated, may hold values from -2 to 2
- visibilities: float32 [16, 2, 8, 16, 256], P('facet', 'grp'), may hold values from -6 to 6
- data_dual: float32 [16, 2, 8, 16, 256], P('facet', 'grp'), may hold values from -6 to 6
- ball_radii: float32 [16, 2, 8], P('facet', 'grp'), may hold values from 19.2 to 256
- blocks: bfloat16 [16, 2, 16, 256, 256], P('facet', 'grp'), may hold values from -0.375 to 0.375
- row_index: int32 [16, 2, 16], P('facet', 'grp'), may hold values from 0 to 7
- col_index: int32 [16, 2, 16], P('facet', 'grp'), may hold values from 0 to 23
Outputs:
- image_out: float32 [16, 256, 256], P(None, 'facet', 'grp')
- data_dual_out: float32 [16, 2, 8, 16, 256], P('facet', 'grp')
- wavelet_dual_out: bfloat16 [8, 16, 256, 256], P(None, None, 'facet', 'grp')
The draws below stay inside these ranges and needn't reach their ends.
Inputs may be any that keep to these rules, and one draw needn't show every extreme that they name: `row_index`: the visibility block of the same device that an operator block feeds. `col_index`: a tile of the band of three facets (the facet above, the device's own, the facet below) over the device's 128 columns, numbered row of tiles by row of tiles, 8 tiles a row.
All inputs are finite; a program needn't handle non-finite values.
Results may differ from the reference program's by a relative error of at most 0.0071.
Values may be sent and summed in bfloat16 or wider, within the bound.
A program may use at most 64 MiB of HBM per device.

```python
import math
import jax
import jax.numpy as jnp
from jax import lax

C = 16
NB = 8
W = 3
TS = 16
ITERS = 2
RF = 16
CG = 128
VB = 256
KDEV = 16
RB = 8
FACETS = 16
GROUPS = 2
NY = 256
NX = 256
PIX = 256
TAPS = 7
NT3 = 24


def with_ends(result, own_key, smallest, high):
    longest = result.shape.index(max(result.shape))
    spots = []
    for shift in (0, 1):
        where = [jax.random.randint(jax.random.fold_in(own_key, axis), (), 0, length) for axis, length in enumerate(result.shape)]
        where[longest] = (where[longest] + shift) % result.shape[longest]
        spots.append(tuple(where))
    return result.at[spots[0]].set(smallest).at[spots[1]].set(high)


def steps_of(own_key, dims, pieces, least, high):
    def one(position, blocks):
        heights = jax.random.uniform(jax.random.fold_in(jax.random.fold_in(own_key, 6), position), (blocks,), jnp.float32, least / len(pieces), high / len(pieces))
        return jnp.repeat(jnp.exp(heights), dims[position] // blocks).reshape((-1,) + (1,) * (len(dims) - position - 1))

    level = one(*pieces[0])
    for cut in pieces[1:]:
        level = level * one(*cut)
    return level


def noise(own_key, extent, scale, bound, pieces=(), kind=jnp.bfloat16):
    entries = jax.random.normal(own_key, extent, jnp.float32) * scale
    if len(pieces) > 0:
        entries = steps_of(own_key, extent, pieces, -0.22, 0.18) * entries
    return jnp.clip(entries, min=-bound, max=bound).astype(kind)


def setup_inputs(seed: int = 0) -> dict:
    arg_keys = jax.random.split(jax.random.key(seed), 11)
    return {
        "image": jnp.clip(2.0 * jax.random.uniform(arg_keys[0], (C, NY, NX), jnp.float32) ** steps_of(arg_keys[0], (C, NY, NX), ((1, 16), (2, 2)), -0.2, 0.2), 0.0, 2.0),
        "wavelet_dual": noise(arg_keys[1], (NB, C, NY, NX), 1.0, 6.0, ((2, 16), (3, 2))),
        "thresholds": jnp.clip(jnp.exp(math.log(10.0) - 2.3025851 * jax.random.uniform(arg_keys[2], (NB, NY, NX), jnp.float32) ** steps_of(arg_keys[2], (NB, NY, NX), ((1, 16), (2, 2)), -0.2, 0.2)), 1.0, 10.0),
        "filter_taps": noise(arg_keys[3], (NB, 2, TAPS), TAPS ** -0.5, 2.0, (), jnp.float32),
        "visibilities": noise(arg_keys[4], (FACETS, GROUPS, RB, C, VB), 1.0, 6.0, ((0, 16), (1, 2)), jnp.float32),
        "data_dual": noise(arg_keys[5], (FACETS, GROUPS, RB, C, VB), 1.0, 6.0, ((0, 16), (1, 2)), jnp.float32),
        "ball_radii": jnp.clip(jnp.exp(math.log(256.0) - 2.5902671 * jax.random.uniform(arg_keys[6], (FACETS, GROUPS, RB), jnp.float32) ** steps_of(arg_keys[6], (FACETS, GROUPS, RB), ((0, 16), (1, 2)), -0.2, 0.2)), 19.2, 256.0),
        "blocks": noise(arg_keys[7], (FACETS, GROUPS, KDEV, PIX, VB), PIX ** -0.5, 0.375, ((0, 16), (1, 2))),
        "row_index": with_ends(jax.random.randint(arg_keys[8], (FACETS, GROUPS, KDEV), 0, RB), jax.random.fold_in(arg_keys[8], 1), 0, RB - 1).astype(jnp.int32),
        "col_index": with_ends(jax.random.randint(arg_keys[9], (FACETS, GROUPS, KDEV), 0, NT3), jax.random.fold_in(arg_keys[9], 1), 0, NT3 - 1).astype(jnp.int32),
    }


step_primal = 0.5
step_data = 0.5
step_wave = 0.5

def tile_coords(col_index):
    per_row = CG // TS
    facet_ids = lax.broadcasted_iota(jnp.int32, col_index.shape, 0)
    group_ids = lax.broadcasted_iota(jnp.int32, col_index.shape, 1)
    tile_rows = facet_ids * (RF // TS) + col_index // per_row
    tile_cols = group_ids * per_row + col_index % per_row
    return (tile_rows.astype(jnp.int32), tile_cols.astype(jnp.int32))

def to_tiles(picture):
    channels, height, width = picture.shape
    shaped = picture.reshape(channels, height // TS, TS, width // TS, TS)
    return shaped.transpose(1, 3, 0, 2, 4).reshape(height // TS, width // TS, channels, TS * TS)

def from_tiles(tile_grid):
    tile_high, tile_wide, channels, pixels = tile_grid.shape
    shaped = tile_grid.reshape(tile_high, tile_wide, channels, TS, TS)
    return shaped.transpose(2, 0, 3, 1, 4).reshape(channels, tile_high * TS, tile_wide * TS)

def measure(picture, blocks, row_index, col_index):
    padded = jnp.pad(picture, ((0, 0), (RF, RF), (0, 0)))
    tile_grid = to_tiles(padded)
    tile_rows, tile_cols = tile_coords(col_index)
    picked = tile_grid[tile_rows, tile_cols]

    def one_facet(inputs):
        tile_set, operators, row_ids = inputs
        products = jnp.einsum('gkcp,gkpv->gkcv', tile_set.astype(jnp.float32), operators.astype(jnp.float32), precision=lax.Precision.HIGHEST)
        selector = (row_ids[:, :, None] == jnp.arange(RB, dtype=jnp.int32)[None, None, :]).astype(jnp.float32)
        return jnp.einsum('gkr,gkcv->grcv', selector, products, precision=lax.Precision.HIGHEST)
    return lax.map(one_facet, (picked, blocks, row_index))

def back_project(duals, blocks, row_index, col_index):
    group_ids = jnp.arange(GROUPS, dtype=jnp.int32)[:, None]

    def one_facet(inputs):
        dual_set, operators, row_ids = inputs
        picked = dual_set[group_ids, row_ids]
        return jnp.einsum('gkcv,gkpv->gkcp', picked.astype(jnp.float32), operators.astype(jnp.float32), precision=lax.Precision.HIGHEST)
    contrib = lax.map(one_facet, (duals, blocks, row_index))
    tile_rows, tile_cols = tile_coords(col_index)
    tile_grid = jnp.zeros(((NY + 2 * RF) // TS, NX // TS, C, TS * TS), jnp.float32)
    tile_grid = tile_grid.at[tile_rows, tile_cols].add(contrib)
    return from_tiles(tile_grid)[:, RF:RF + NY, :]

def analysis(picture, taps):
    height, width = (picture.shape[1], picture.shape[2])
    padded = jnp.pad(picture, ((0, 0), (W, W), (W, W)))
    row_sums = jnp.zeros((picture.shape[0], height, width + 2 * W), jnp.float32)
    for tap in range(TAPS):
        row_sums = row_sums + taps[0, tap] * padded[:, tap:tap + height, :]
    total = jnp.zeros(picture.shape, jnp.float32)
    for tap in range(TAPS):
        total = total + taps[1, tap] * row_sums[:, :, tap:tap + width]
    return total

def synthesis(duals, taps):
    height, width = (duals.shape[1], duals.shape[2])
    padded = jnp.pad(duals, ((0, 0), (W, W), (W, W)))
    row_sums = jnp.zeros((duals.shape[0], height, width + 2 * W), jnp.float32)
    for tap in range(TAPS):
        row_sums = row_sums + taps[0, tap] * padded[:, 2 * W - tap:2 * W - tap + height, :]
    total = jnp.zeros(duals.shape, jnp.float32)
    for tap in range(TAPS):
        total = total + taps[1, tap] * row_sums[:, :, 2 * W - tap:2 * W - tap + width]
    return total

def reference(image, wavelet_dual, thresholds, filter_taps, visibilities, data_dual, ball_radii, blocks, row_index, col_index):
    primal = image
    dual_data = data_dual
    dual_wave = wavelet_dual
    for iteration in range(ITERS):
        backward = back_project(dual_data.astype(jnp.bfloat16), blocks, row_index, col_index)
        smooth = jnp.zeros(primal.shape, jnp.float32)
        for basis in range(NB):
            smooth = smooth + synthesis(dual_wave[basis].astype(jnp.float32), filter_taps[basis])
        updated = jnp.maximum(primal - step_primal * (backward + smooth), 0.0)
        extrap = (2.0 * updated - primal).astype(jnp.bfloat16)
        prediction = measure(extrap, blocks, row_index, col_index)
        moved = dual_data + step_data * prediction
        offset = moved / step_data - visibilities
        length = jnp.sqrt(lax.optimization_barrier(jnp.sum(offset * offset, axis=(3, 4))))
        nearest = visibilities + offset * (ball_radii / jnp.maximum(length, ball_radii))[..., None, None]
        dual_data = moved - step_data * nearest
        extrap_wide = extrap.astype(jnp.float32)
        new_wave = []
        for basis in range(NB):
            widened = dual_wave[basis].astype(jnp.float32) + step_wave * analysis(extrap_wide, filter_taps[basis])
            magnitude = jnp.sqrt(lax.optimization_barrier(jnp.sum(widened * widened, axis=0)))
            shrink = thresholds[basis] / jnp.maximum(magnitude, thresholds[basis])
            new_wave.append((widened * shrink[None]).astype(jnp.bfloat16))
        dual_wave = jnp.stack(new_wave)
        primal = updated
    return (primal, dual_data, dual_wave)
```

```python
import functools

import jax
import jax.numpy as jnp
from jax import lax
from jax.experimental import pallas as pl
from jax.experimental.pallas import tpu as pltpu
from jax.sharding import PartitionSpec as P

W = 3
TS = 16
ITERS = 2
MESH = pl.DeviceIdType.MESH
F32 = jnp.float32
BF16 = jnp.bfloat16
ROWS = ((-1, 0), (1, 0))
SIDES = ((0, -1), (0, 1), (-1, -1), (-1, 1), (1, -1), (1, 1))
DIRS = ROWS + SIDES
ROW_SLOT = {0: 0, 1: 1, -1: 2}
SIDE_SLOT = {1: 0, -1: 1}


def iota(shape, dim):
    return lax.broadcasted_iota(jnp.int32, shape, dim)


def tap_matrix(position, taps):
    out = jnp.zeros(position.shape, F32)
    for tap, value in enumerate(taps):
        out = jnp.where(position == tap, value, out)
    return out


def swap_groups(items):
    count = len(items)
    lanes = items[0].shape[-1]
    group = iota(items[0].shape, 1) // TS
    step = count // 2
    while step:
        low = (group // step) % 2 == 0
        out = list(items)
        for a in range(count):
            if (a // step) % 2 == 0:
                first, second = items[a], items[a + step]
                out[a] = jnp.where(low, first, pltpu.roll(second, step * TS, 1))
                out[a + step] = jnp.where(low, pltpu.roll(first, lanes - step * TS, 1), second)
        items = out
        step //= 2
    return items


def kernel(
    sizes,
    image, dual_wave, thresholds, taps, seen, dual_data, radius, blocks, row_ids, col_ids,
    image_out, data_out, wave_out,
    u_in, ops, thr, vis, vdat, ttap, stap, rtap, ptap, ycols, rfilt,
    near, zrim, ztile, zedge, zedge_own, rim_own, rim, edge_own, edge, tsum_own, tsum,
    parts, uslot, vslot, xslot, turn,
    local_sem, send_sem, recv_sem,
):
    nf, ng, NB, C, R, L, KB, RB, PIX, VB, TAPS, NT3 = sizes
    f = lax.axis_index("facet")
    g = lax.axis_index("grp")
    T1 = L // TS
    LC = C * L
    EW = L // C

    def exists(d):
        df, dg = d
        ok = None
        for test in ([f > 0] if df < 0 else [f < nf - 1] if df > 0 else []) + (
            [g > 0] if dg < 0 else [g < ng - 1] if dg > 0 else []
        ):
            ok = test if ok is None else jnp.logical_and(ok, test)
        return ok

    def back(d):
        return (-d[0], -d[1])

    def where_to(d):
        return {"facet": f + d[0], "grp": g + d[1]}

    loads = [
        pltpu.make_async_copy(src, dst, local_sem.at[n])
        for n, (src, dst) in enumerate(
            ((dual_wave, u_in), (dual_data, vdat), (blocks, ops), (seen, vis), (thresholds, thr))
        )
    ]
    for load in loads:
        load.start()

    for ref in (rim, edge, tsum, near, zedge):
        ref[...] = jnp.zeros(ref.shape, ref.dtype)
    for it in range(ITERS):
        ztile[it, :T1] = jnp.zeros((T1, C, PIX), BF16)
        ztile[it, 2 * T1 :] = jnp.zeros((T1, C, PIX), BF16)

    barrier = pltpu.get_barrier_semaphore()
    for d in DIRS:
        @pl.when(exists(d))
        def _(d=d):
            pl.semaphore_signal(barrier, inc=1, device_id=where_to(d), device_id_type=MESH)

    src = iota((L, L), 0)
    dst = iota((L, L), 1)
    m_dst = dst % EW
    m_src = src % EW
    over = jnp.where(m_dst < W, m_dst - W, jnp.where(m_dst < 2 * W, L + m_dst - W, 4 * L))
    halo = jnp.where(m_src < W, L + m_src, jnp.where(m_src < 2 * W, m_src - 2 * W, 4 * L))
    row_out = iota((2 * R, NB * R), 0)
    row_out = jnp.where(row_out < R, row_out, jnp.where(row_out < R + W, row_out - R - W, jnp.where(row_out < R + 2 * W, row_out - W, 4 * L)))
    row_in = iota((2 * R, NB * R), 1)
    row_at = iota((R, 3 * R), 1)
    row_at = jnp.where(row_at < R, row_at, jnp.where(row_at < 2 * R, row_at - 2 * R, row_at - R))
    row_to = iota((R, 3 * R), 0)
    synth_rows = jnp.zeros((2 * R, NB * R), F32)
    for b in range(NB):
        rt = [taps[b, 0, t] for t in range(TAPS)]
        ct = [taps[b, 1, t] for t in range(TAPS)]
        ch = [0.5 * t for t in ct]
        stap[b, :, :L] = tap_matrix(dst + W - src, ct).astype(BF16)
        stap[b, :, L:] = tap_matrix(over + W - src, ct).astype(BF16)
        ttap[b, :L] = tap_matrix(src - dst + W, ch).astype(BF16)
        ttap[b, L:] = tap_matrix(halo - dst + W, ch).astype(BF16)
        rtap[b * R : (b + 1) * R] = tap_matrix(row_at - row_to + W, rt).astype(BF16)
        synth_rows = jnp.where(row_in // R == b, tap_matrix(row_out + W - (row_in - b * R), rt), synth_rows)
    ptap[...] = synth_rows.astype(BF16)
    pick = jnp.where(jnp.logical_or(jnp.logical_and(m_dst < W, src == m_dst), jnp.logical_and(jnp.logical_and(m_dst >= W, m_dst < 2 * W), src == L - 2 * W + m_dst)), 1.0, 0.0).astype(BF16)
    place = jnp.where(jnp.logical_or(jnp.logical_and(m_src < W, dst == L - W + m_src), jnp.logical_and(jnp.logical_and(m_src >= W, m_src < 2 * W), dst == m_src - W)), 1.0, 0.0).astype(BF16)
    q_to = iota((R, 2 * R), 0)
    q_at = iota((R, 2 * R), 1)
    settle = jnp.where(jnp.logical_or(jnp.logical_and(q_to < W, q_at == q_to + W), jnp.logical_and(q_to >= R - W, q_at == q_to + W)), 1.0, 0.0).astype(BF16)
    lane_c = iota((R, L), 1) // EW
    lane_m = iota((R, L), 1) % EW

    def dot(a, b):
        return jnp.dot(a, b, preferred_element_type=F32)

    tall = 3 - (f == 0).astype(jnp.int32) - (f == nf - 1).astype(jnp.int32)
    wide = 3 - (g == 0).astype(jnp.int32) - (g == ng - 1).astype(jnp.int32)
    pl.semaphore_wait(barrier, tall * wide - 1)

    sent = []

    def message(it, kind, d, src_ref, dst_ref):
        slot = (it * 4 + kind) * 8 + DIRS.index(d)
        return pltpu.make_async_remote_copy(
            src_ref=src_ref, dst_ref=dst_ref, send_sem=send_sem.at[slot], recv_sem=recv_sem.at[slot],
            device_id=where_to(d), device_id_type=MESH,
        )

    def send(copies):
        for d, copy in copies:
            pl.when(exists(d))(copy.start)
        sent.extend(copies)

    def receive(copies):
        for d, copy in copies:
            pl.when(exists(back(d)))(copy.wait_recv)

    loads[0].wait()
    for it in range(ITERS):
        for b in range(NB):
            cells = (u_in[b] if it == 0 else uslot[b]).reshape(C * R, L)
            cols = dot(cells, stap[b])
            rimc = jnp.zeros((R, L), F32)
            for c in range(C):
                part = cols[c * R : (c + 1) * R]
                ycols[b * R : (b + 1) * R, c * L : (c + 1) * L] = part[:, :L].astype(BF16)
                rimc = jnp.where(lane_c == c, part[:, L:], rimc)
            ycols[b * R : (b + 1) * R, LC:] = rimc.astype(BF16)
        smooth = dot(ptap[...], ycols[...])
        rim_own[it] = smooth[R:, :LC].astype(BF16)
        edge_own[it] = smooth[:, LC:].astype(BF16).reshape(2, R, L)
        xslot[...] = smooth[:R, :LC]
        msg_a = [(d, message(it, 0, d, rim_own.at[it], rim.at[it, ROW_SLOT[d[0]] - 1])) for d in ROWS]
        msg_a += [
            (d, message(it, 0, d, edge_own.at[it, 0 if d[0] == 0 else 1], edge.at[it, SIDE_SLOT[d[1]], ROW_SLOT[d[0]]]))
            for d in SIDES
        ]
        send(msg_a)

        if it == 0:
            loads[1].wait()
            for r in range(RB):
                turn[r] = vdat[0, 0, r].astype(BF16)
            loads[2].wait()
        for k in range(KB):
            parts[k] = lax.dot_general(
                turn[row_ids[0, 0, k]], ops[0, 0, k], (((1,), (1,)), ((), ())), preferred_element_type=F32
            )

        def tile_total(q):
            total = jnp.where(col_ids[0, 0, 0] == q, 1.0, 0.0) * parts[0]
            for k in range(1, KB):
                total = total + jnp.where(col_ids[0, 0, k] == q, 1.0, 0.0) * parts[k]
            return total

        for t in range(T1):
            tsum_own[it, 0, t] = tile_total(t).astype(BF16)
            tsum_own[it, 1, t] = tile_total(2 * T1 + t).astype(BF16)
        msg_b = [
            (d, message(it, 1, d, tsum_own.at[it, 0 if d[0] < 0 else 1], tsum.at[it, ROW_SLOT[d[0]] - 1])) for d in ROWS
        ]
        send(msg_b)
        totals = [tile_total(T1 + t) for t in range(T1)]

        receive(msg_a)
        rows_in = dot(settle, rim[it].reshape(2 * R, LC))
        came = [jnp.where(lane_m >= W, edge[it, 0, s].astype(F32), edge[it, 1, s].astype(F32)) for s in range(3)]
        corner = dot(settle, jnp.concatenate([came[1], came[2]], axis=0).astype(BF16))
        side = came[0] + corner
        spread = jnp.concatenate([jnp.where(lane_c == c, side, 0.0) for c in range(C)], axis=0).astype(BF16)
        side_in = dot(spread, place)
        receive(msg_b)
        totals = [totals[t] + (tsum[it, 0, t].astype(F32) + tsum[it, 1, t].astype(F32)) for t in range(T1)]
        lines = []
        for h in range(PIX // L):
            lines += swap_groups([t[:, h * L : (h + 1) * L] for t in totals])
        backward = jnp.swapaxes(jnp.stack(lines), 0, 1)

        extrap = []
        for c in range(C):
            here = slice(c * L, (c + 1) * L)
            old = image[c] if it == 0 else vslot[c]
            grad = backward[c] + (xslot[:, here] + rows_in[:, here] + side_in[c * R : (c + 1) * R])
            new = jnp.maximum(old - 0.5 * grad, 0.0)
            if it == ITERS - 1:
                image_out[c] = new
            else:
                vslot[c] = new
            ext = (2.0 * new - old).astype(BF16)
            near[it, 0, :, here] = ext
            extrap.append(ext)
        msg_c = [(d, message(it, 2, d, near.at[it, 0], near.at[it, ROW_SLOT[d[0]]])) for d in ROWS]
        flat = jnp.concatenate(extrap, axis=0)
        edges = dot(flat, pick)
        mine = jnp.zeros((R, L), F32)
        for c in range(C):
            mine = jnp.where(lane_c == c, edges[c * R : (c + 1) * R], mine)
        zedge_own[it] = mine.astype(BF16)
        msg_c += [
            (d, message(it, 2, d, zedge_own.at[it], zedge.at[it, SIDE_SLOT[d[1]], ROW_SLOT[d[0]]])) for d in SIDES
        ]
        send(msg_c)
        turned = jnp.swapaxes(flat.astype(F32).reshape(C, R, L), 0, 1)
        for h in range(PIX // L):
            tiles = swap_groups([turned[h * T1 + i] for i in range(T1)])
            for t in range(T1):
                ztile[it, T1 + t, :, h * L : (h + 1) * L] = tiles[t].astype(BF16)
        own_tiles = ztile.at[it, pl.ds(T1, T1)]
        msg_d = [
            (d, message(it, 3, d, own_tiles, ztile.at[it, pl.ds(2 * T1 if d[0] < 0 else 0, T1)])) for d in ROWS
        ]
        send(msg_d)

        receive(msg_c)
        zside = [jnp.where(lane_m >= W, zedge[it, 0, s].astype(F32), zedge[it, 1, s].astype(F32)) for s in range(3)]
        zside = jnp.concatenate(zside, axis=0).astype(BF16)
        side_rows = dot(rtap[...], zside)
        for c in range(C):
            lines_c = dot(rtap[...], near[it, :, :, c * L : (c + 1) * L].reshape(3 * R, L)).astype(BF16)
            side_c = jnp.where(iota((NB * R, L), 1) // EW == c, side_rows, 0.0).astype(BF16)
            rfilt[:, c, :, :L] = lines_c.reshape(NB, R, L)
            rfilt[:, c, :, L:] = side_c.reshape(NB, R, L)
        if it == 0:
            loads[4].wait()
        for b in range(NB):
            half = dot(rfilt[b].reshape(C * R, 2 * L), ttap[b]).reshape(C, R, L)
            cells = (u_in[b] if it == 0 else uslot[b]).astype(F32)
            widened = cells + half
            magnitude = jnp.sqrt(jnp.sum(widened * widened, axis=0))
            bound = thr[b]
            shrink = bound / jnp.maximum(magnitude, bound)
            new_u = (widened * shrink[None]).astype(BF16)
            if it == ITERS - 1:
                wave_out[b] = new_u
            else:
                uslot[b] = new_u

        receive(msg_d)
        for k in range(KB):
            parts[k] = dot(ztile[it, col_ids[0, 0, k]], ops[0, 0, k])
        if it == 0:
            loads[3].wait()
        for r in range(RB):
            pred = jnp.where(row_ids[0, 0, 0] == r, 1.0, 0.0) * parts[0]
            for k in range(1, KB):
                pred = pred + jnp.where(row_ids[0, 0, k] == r, 1.0, 0.0) * parts[k]
            moved = (vdat[0, 0, r] if it == 0 else data_out[0, 0, r]) + 0.5 * pred
            offset = 2.0 * moved - vis[0, 0, r]
            length = jnp.sqrt(jnp.sum(jnp.sum(offset * offset, axis=0, keepdims=True), axis=1, keepdims=True))
            ball = radius[0, 0, r]
            nearest = vis[0, 0, r] + offset * (ball / jnp.maximum(length, ball))
            new_v = moved - 0.5 * nearest
            data_out[0, 0, r] = new_v
            turn[r] = new_v.astype(BF16)

    for d, copy in sent:
        pl.when(exists(d))(copy.wait_send)


def solution(mesh):
    nf, ng = mesh.shape["facet"], mesh.shape["grp"]

    def per_device(image, dual_wave, thresholds, taps, seen, dual_data, radius, blocks, row_ids, col_ids):
        C, R, L = image.shape
        NB, _, TAPS = taps.shape
        KB, PIX, VB = blocks.shape[2:]
        RB = seen.shape[2]
        T1 = L // TS
        sizes = (nf, ng, NB, C, R, L, KB, RB, PIX, VB, TAPS, 3 * T1)
        vmem = pl.BlockSpec(memory_space=pltpu.VMEM)
        smem = pl.BlockSpec(memory_space=pltpu.SMEM)
        hbm = pl.BlockSpec(memory_space=pl.ANY)
        V = pltpu.VMEM
        messages = ITERS * 4 * 8
        return pl.pallas_call(
            functools.partial(kernel, sizes),
            out_shape=(
                jax.ShapeDtypeStruct(image.shape, F32),
                jax.ShapeDtypeStruct(dual_data.shape, F32),
                jax.ShapeDtypeStruct(dual_wave.shape, BF16),
            ),
            in_specs=[vmem, hbm, hbm, smem, hbm, hbm, smem, hbm, smem, smem],
            out_specs=(vmem, vmem, vmem),
            scratch_shapes=[
                V(dual_wave.shape, BF16),
                V(blocks.shape, BF16),
                V(thresholds.shape, F32),
                V(seen.shape, F32),
                V(dual_data.shape, F32),
                V((NB, 2 * L, L), BF16),
                V((NB, L, 2 * L), BF16),
                V((NB * R, 3 * R), BF16),
                V((2 * R, NB * R), BF16),
                V((NB * R, C * L + L), BF16),
                V((NB, C, R, 2 * L), BF16),
                V((ITERS, 3, R, C * L), BF16),
                V((8, 128), BF16),
                V((ITERS, 3 * T1, C, PIX), BF16),
                V((ITERS, 2, 3, R, L), BF16),
                V((ITERS, R, L), BF16),
                V((ITERS, R, C * L), BF16),
                V((ITERS, 2, R, C * L), BF16),
                V((ITERS, 2, R, L), BF16),
                V((ITERS, 2, 3, R, L), BF16),
                V((ITERS, 2, T1, C, PIX), BF16),
                V((ITERS, 2, T1, C, PIX), BF16),
                V((KB, C, max(PIX, VB)), F32),
                V(dual_wave.shape, BF16),
                V(image.shape, F32),
                V((R, C * L), F32),
                V((RB, C, VB), BF16),
                pltpu.SemaphoreType.DMA((5,)),
                pltpu.SemaphoreType.DMA((messages,)),
                pltpu.SemaphoreType.DMA((messages,)),
            ],
            compiler_params=pltpu.CompilerParams(collective_id=0, has_side_effects=True, vmem_limit_bytes=60 << 20),
        )(image, dual_wave, thresholds, taps, seen, dual_data, radius, blocks, row_ids, col_ids)

    dev = P("facet", "grp")
    rows = P(None, "facet", "grp")
    wave = P(None, None, "facet", "grp")
    return jax.shard_map(
        per_device,
        mesh=mesh,
        in_specs=(rows, wave, rows, P(), dev, dev, dev, dev, dev, dev),
        out_specs=(rows, dev, wave),
        check_vma=False,
    )
```

```python
import functools

import jax
import jax.numpy as jnp
from jax import lax
from jax.experimental import pallas as pl
from jax.experimental.pallas import tpu as pltpu
from jax.sharding import PartitionSpec as P

W = 3
TS = 16
ITERS = 2
MESH = pl.DeviceIdType.MESH
F32 = jnp.float32
BF16 = jnp.bfloat16
ROWS = ((-1, 0), (1, 0))
SIDES = ((0, -1), (0, 1), (-1, -1), (-1, 1), (1, -1), (1, 1))
DIRS = ROWS + SIDES
ROW_SLOT = {0: 0, 1: 1, -1: 2}
SIDE_SLOT = {1: 0, -1: 1}


def iota(shape, dim):
    return lax.broadcasted_iota(jnp.int32, shape, dim)


def tap_matrix(position, taps):
    out = jnp.zeros(position.shape, F32)
    for tap, value in enumerate(taps):
        out = jnp.where(position == tap, value, out)
    return out


def swap_groups(items):
    count = len(items)
    lanes = items[0].shape[-1]
    group = iota(items[0].shape, 1) // TS
    step = count // 2
    while step:
        low = (group // step) % 2 == 0
        out = list(items)
        for a in range(count):
            if (a // step) % 2 == 0:
                first, second = items[a], items[a + step]
                out[a] = jnp.where(low, first, pltpu.roll(second, step * TS, 1))
                out[a + step] = jnp.where(low, pltpu.roll(first, lanes - step * TS, 1), second)
        items = out
        step //= 2
    return items


def kernel(
    sizes,
    image, dual_wave, thresholds, taps, seen, dual_data, radius, blocks, row_ids, col_ids,
    image_out, data_out, wave_out,
    u_in, ops, thr, vis, vdat, ttap, stap, rtap, ptap, ycols, rfilt,
    near, zrim, ztile, zedge, zedge_own, rim_own, rim, edge_own, edge, tsum_own, tsum,
    parts, uslot, vslot, xslot, turn, links,
    local_sem, send_sem, recv_sem,
):
    nf, ng, NB, C, R, L, KB, RB, PIX, VB, TAPS, NT3 = sizes
    f = lax.axis_index("facet")
    g = lax.axis_index("grp")
    T1 = L // TS
    LC = C * L
    EW = L // C

    def exists(d):
        df, dg = d
        ok = None
        for test in ([f > 0] if df < 0 else [f < nf - 1] if df > 0 else []) + (
            [g > 0] if dg < 0 else [g < ng - 1] if dg > 0 else []
        ):
            ok = test if ok is None else jnp.logical_and(ok, test)
        return ok

    def back(d):
        return (-d[0], -d[1])

    def where_to(d):
        return {"facet": f + d[0], "grp": g + d[1]}

    loads = [
        pltpu.make_async_copy(src, dst, local_sem.at[n])
        for n, (src, dst) in enumerate(
            ((dual_wave, u_in), (dual_data, vdat), (blocks, ops), (seen, vis), (thresholds, thr))
        )
    ]
    for load in loads:
        load.start()

    for ref in (rim, edge, tsum, near, zedge):
        ref[...] = jnp.zeros(ref.shape, ref.dtype)
    for it in range(ITERS):
        ztile[it, :T1] = jnp.zeros((T1, C, PIX), BF16)
        ztile[it, 2 * T1 :] = jnp.zeros((T1, C, PIX), BF16)

    barrier = pltpu.get_barrier_semaphore()
    for d in DIRS:
        @pl.when(exists(d))
        def _(d=d):
            pl.semaphore_signal(barrier, inc=1, device_id=where_to(d), device_id_type=MESH)

    src = iota((L, L), 0)
    dst = iota((L, L), 1)
    m_dst = dst % EW
    m_src = src % EW
    row_out = iota((2 * R, NB * R), 0)
    row_out = jnp.where(row_out < R, row_out, jnp.where(row_out < R + W, row_out - R - W, jnp.where(row_out < R + 2 * W, row_out - W, 4 * L)))
    row_in = iota((2 * R, NB * R), 1)
    row_at = iota((R, 3 * R), 1)
    row_at = jnp.where(row_at < R, row_at, jnp.where(row_at < 2 * R, row_at - 2 * R, row_at - R))
    row_to = iota((R, 3 * R), 0)
    synth_rows = jnp.zeros((2 * R, NB * R), F32)
    sub, lane = iota((EW, L), 0), iota((EW, L), 1)
    last_sub = sub + L - EW
    m_lane = lane % EW
    over_col = jnp.where(m_lane < W, m_lane - W, jnp.where(m_lane < 2 * W, L + m_lane - W, 4 * L))
    halo_col = jnp.where(sub < W, L + sub, jnp.where(sub < 2 * W, sub - 2 * W, 4 * L))
    none = jnp.zeros((EW, L), F32)

    def band(values, sign):
        ahead = (sign * (lane - sub) + W + L) % L
        base = tap_matrix(ahead, values)
        pieces = [base] + [pltpu.roll(base, n * EW, 1) for n in range(1, C)]
        pieces[0] = jnp.where(lane < L // 2, base, 0.0)
        pieces[-1] = jnp.where(lane < L // 2, 0.0, pieces[-1])
        return pieces

    def store(ref, b, row, col, pieces, low=False):
        for n in range(0, len(pieces), 2):
            value = jnp.concatenate(pieces[n : n + 2], axis=0)
            high = value.astype(BF16)
            ref[b, row + n * EW : row + (n + 2) * EW, col : col + L] = high
            if low:
                rest = (value - high.astype(F32)).astype(BF16)
                ref[b, row + L + n * EW : row + L + (n + 2) * EW, col : col + L] = rest

    for b in range(NB):
        rt = [taps[t, 0, b] for t in range(TAPS)]
        ct = [taps[t, 1, b] for t in range(TAPS)]
        ch = [0.5 * t for t in ct]
        store(stap, b, 0, 0, band(ct, 1), True)
        rim_first = tap_matrix(over_col + W - sub, ct)
        rim_last = tap_matrix(over_col + W - last_sub, ct)
        store(stap, b, 0, L, [rim_first] + [none] * (C - 2) + [rim_last], True)
        store(ttap, b, 0, 0, band(ch, -1))
        store(ttap, b, L, 0, [tap_matrix(halo_col - lane + W, ch)] * C)
        rtap[b * R : (b + 1) * R] = tap_matrix(row_at - row_to + W, rt).astype(BF16)
        synth_rows = jnp.where(row_in // R == b, tap_matrix(row_out + W - (row_in - b * R), rt), synth_rows)
    rows_high = synth_rows.astype(BF16)
    ptap[: 2 * R] = rows_high
    ptap[2 * R :] = (synth_rows - rows_high.astype(F32)).astype(BF16)
    for side, (ids, count) in enumerate(((col_ids, NT3), (row_ids, RB))):
        for k in range(KB):
            before = KB
            for j in range(k):
                before = jnp.where(ids[0, 0, j] == ids[0, 0, k], j, before)
            links[2 * side, k] = before
        for q in range(count):
            last = KB
            for k in range(KB):
                last = jnp.where(ids[0, 0, k] == q, k, last)
            links[2 * side + 1, q] = last
    parts[KB] = jnp.zeros(parts.shape[1:], F32)
    pick = jnp.where(jnp.logical_or(jnp.logical_and(m_dst < W, src == m_dst), jnp.logical_and(jnp.logical_and(m_dst >= W, m_dst < 2 * W), src == L - 2 * W + m_dst)), 1.0, 0.0).astype(BF16)
    place = jnp.where(jnp.logical_or(jnp.logical_and(m_src < W, dst == L - W + m_src), jnp.logical_and(jnp.logical_and(m_src >= W, m_src < 2 * W), dst == m_src - W)), 1.0, 0.0).astype(BF16)
    q_to = iota((R, 2 * R), 0)
    q_at = iota((R, 2 * R), 1)
    settle = jnp.where(jnp.logical_or(jnp.logical_and(q_to < W, q_at == q_to + W), jnp.logical_and(q_to >= R - W, q_at == q_to + W)), 1.0, 0.0).astype(BF16)
    lane_c = iota((R, L), 1) // EW
    lane_m = iota((R, L), 1) % EW

    def dot(a, b):
        return jnp.dot(a, b, preferred_element_type=F32)

    tall = 3 - (f == 0).astype(jnp.int32) - (f == nf - 1).astype(jnp.int32)
    wide = 3 - (g == 0).astype(jnp.int32) - (g == ng - 1).astype(jnp.int32)
    pl.semaphore_wait(barrier, tall * wide - 1)

    sent = []

    def message(it, kind, d, src_ref, dst_ref):
        slot = (it * 4 + kind) * 8 + DIRS.index(d)
        return pltpu.make_async_remote_copy(
            src_ref=src_ref, dst_ref=dst_ref, send_sem=send_sem.at[slot], recv_sem=recv_sem.at[slot],
            device_id=where_to(d), device_id_type=MESH,
        )

    def send(copies):
        for d, copy in copies:
            pl.when(exists(d))(copy.start)
        sent.extend(copies)

    def receive(copies):
        for d, copy in copies:
            pl.when(exists(back(d)))(copy.wait_recv)

    loads[0].wait()
    for it in range(ITERS):
        for b in range(NB):
            cells = (u_in[b] if it == 0 else uslot[b]).reshape(C * R, L)
            cols = dot(jnp.concatenate([cells, cells], axis=1), stap[b])
            rimc = jnp.zeros((R, L), F32)
            for c in range(C):
                part = cols[c * R : (c + 1) * R]
                ycols[b * R : (b + 1) * R, c * L : (c + 1) * L] = part[:, :L].astype(BF16)
                rimc = jnp.where(lane_c == c, part[:, L:], rimc)
            ycols[b * R : (b + 1) * R, LC:] = rimc.astype(BF16)
        smooth = dot(ptap[...], ycols[...])
        smooth = smooth[: 2 * R] + smooth[2 * R :]
        rim_own[it] = smooth[R:, :LC].astype(BF16)
        edge_own[it] = smooth[:, LC:].astype(BF16).reshape(2, R, L)
        xslot[...] = smooth[:R, :LC]
        msg_a = [(d, message(it, 0, d, rim_own.at[it], rim.at[it, ROW_SLOT[d[0]] - 1])) for d in ROWS]
        msg_a += [
            (d, message(it, 0, d, edge_own.at[it, 0 if d[0] == 0 else 1], edge.at[it, SIDE_SLOT[d[1]], ROW_SLOT[d[0]]]))
            for d in SIDES
        ]
        send(msg_a)

        if it == 0:
            loads[1].wait()
            for r in range(RB):
                turn[r] = vdat[0, 0, r].astype(BF16)
            loads[2].wait()
        for k in range(KB):
            part = lax.dot_general(
                turn[row_ids[0, 0, k]], ops[0, 0, k], (((1,), (1,)), ((), ())), preferred_element_type=F32
            )
            parts[k] = part + parts[links[0, k]] if k else part

        def tile_total(q):
            return parts[links[1, q]]

        for t in range(T1):
            tsum_own[it, 0, t] = tile_total(t).astype(BF16)
            tsum_own[it, 1, t] = tile_total(2 * T1 + t).astype(BF16)
        msg_b = [
            (d, message(it, 1, d, tsum_own.at[it, 0 if d[0] < 0 else 1], tsum.at[it, ROW_SLOT[d[0]] - 1])) for d in ROWS
        ]
        send(msg_b)
        totals = [tile_total(T1 + t) for t in range(T1)]

        receive(msg_a)
        rows_in = dot(settle, rim[it].reshape(2 * R, LC))
        came = [jnp.where(lane_m >= W, edge[it, 0, s].astype(F32), edge[it, 1, s].astype(F32)) for s in range(3)]
        corner = dot(settle, jnp.concatenate([came[1], came[2]], axis=0).astype(BF16))
        side = came[0] + corner
        spread = jnp.concatenate([jnp.where(lane_c == c, side, 0.0) for c in range(C)], axis=0).astype(BF16)
        side_in = dot(spread, place)
        receive(msg_b)
        totals = [totals[t] + (tsum[it, 0, t].astype(F32) + tsum[it, 1, t].astype(F32)) for t in range(T1)]
        lines = []
        for h in range(PIX // L):
            lines += swap_groups([t[:, h * L : (h + 1) * L] for t in totals])
        backward = jnp.swapaxes(jnp.stack(lines), 0, 1)

        extrap = []
        for c in range(C):
            here = slice(c * L, (c + 1) * L)
            old = image[c] if it == 0 else vslot[c]
            grad = backward[c] + (xslot[:, here] + rows_in[:, here] + side_in[c * R : (c + 1) * R])
            new = jnp.maximum(old - 0.5 * grad, 0.0)
            if it == ITERS - 1:
                image_out[c] = new
            else:
                vslot[c] = new
            ext = (2.0 * new - old).astype(BF16)
            near[it, 0, :, here] = ext
            extrap.append(ext)
        msg_c = [(d, message(it, 2, d, near.at[it, 0], near.at[it, ROW_SLOT[d[0]]])) for d in ROWS]
        flat = jnp.concatenate(extrap, axis=0)
        edges = dot(flat, pick)
        mine = jnp.zeros((R, L), F32)
        for c in range(C):
            mine = jnp.where(lane_c == c, edges[c * R : (c + 1) * R], mine)
        zedge_own[it] = mine.astype(BF16)
        msg_c += [
            (d, message(it, 2, d, zedge_own.at[it], zedge.at[it, SIDE_SLOT[d[1]], ROW_SLOT[d[0]]])) for d in SIDES
        ]
        send(msg_c)
        turned = jnp.swapaxes(flat.astype(F32).reshape(C, R, L), 0, 1)
        for h in range(PIX // L):
            tiles = swap_groups([turned[h * T1 + i] for i in range(T1)])
            for t in range(T1):
                ztile[it, T1 + t, :, h * L : (h + 1) * L] = tiles[t].astype(BF16)
        own_tiles = ztile.at[it, pl.ds(T1, T1)]
        msg_d = [
            (d, message(it, 3, d, own_tiles, ztile.at[it, pl.ds(2 * T1 if d[0] < 0 else 0, T1)])) for d in ROWS
        ]
        send(msg_d)

        receive(msg_c)
        zside = [jnp.where(lane_m >= W, zedge[it, 0, s].astype(F32), zedge[it, 1, s].astype(F32)) for s in range(3)]
        zside = jnp.concatenate(zside, axis=0).astype(BF16)
        side_rows = dot(rtap[...], zside)
        for c in range(C):
            lines_c = dot(rtap[...], near[it, :, :, c * L : (c + 1) * L].reshape(3 * R, L)).astype(BF16)
            side_c = jnp.where(iota((NB * R, L), 1) // EW == c, side_rows, 0.0).astype(BF16)
            rfilt[:, c, :, :L] = lines_c.reshape(NB, R, L)
            rfilt[:, c, :, L:] = side_c.reshape(NB, R, L)
        if it == 0:
            loads[4].wait()
        for b in range(NB):
            half = dot(rfilt[b].reshape(C * R, 2 * L), ttap[b]).reshape(C, R, L)
            cells = (u_in[b] if it == 0 else uslot[b]).astype(F32)
            widened = cells + half
            magnitude = jnp.sqrt(jnp.sum(widened * widened, axis=0))
            bound = thr[b]
            shrink = bound / jnp.maximum(magnitude, bound)
            new_u = (widened * shrink[None]).astype(BF16)
            if it == ITERS - 1:
                wave_out[b] = new_u
            else:
                uslot[b] = new_u

        receive(msg_d)
        for k in range(KB):
            part = dot(ztile[it, col_ids[0, 0, k]], ops[0, 0, k])
            parts[k] = part + parts[links[2, k]] if k else part
        if it == 0:
            loads[3].wait()
        for r in range(RB):
            pred = parts[links[3, r]]
            moved = (vdat[0, 0, r] if it == 0 else data_out[0, 0, r]) + 0.5 * pred
            offset = 2.0 * moved - vis[0, 0, r]
            length = jnp.sqrt(jnp.sum(jnp.sum(offset * offset, axis=0, keepdims=True), axis=1, keepdims=True))
            ball = radius[0, 0, r]
            nearest = vis[0, 0, r] + offset * (ball / jnp.maximum(length, ball))
            new_v = moved - 0.5 * nearest
            data_out[0, 0, r] = new_v
            turn[r] = new_v.astype(BF16)

    for d, copy in sent:
        pl.when(exists(d))(copy.wait_send)


def solution(mesh):
    nf, ng = mesh.shape["facet"], mesh.shape["grp"]

    def per_device(image, dual_wave, thresholds, taps, seen, dual_data, radius, blocks, row_ids, col_ids):
        taps = jnp.transpose(taps, (2, 1, 0))
        C, R, L = image.shape
        TAPS, _, NB = taps.shape
        KB, PIX, VB = blocks.shape[2:]
        RB = seen.shape[2]
        T1 = L // TS
        sizes = (nf, ng, NB, C, R, L, KB, RB, PIX, VB, TAPS, 3 * T1)
        vmem = pl.BlockSpec(memory_space=pltpu.VMEM)
        smem = pl.BlockSpec(memory_space=pltpu.SMEM)
        hbm = pl.BlockSpec(memory_space=pl.ANY)
        V = pltpu.VMEM
        messages = ITERS * 4 * 8
        return pl.pallas_call(
            functools.partial(kernel, sizes),
            out_shape=(
                jax.ShapeDtypeStruct(image.shape, F32),
                jax.ShapeDtypeStruct(dual_data.shape, F32),
                jax.ShapeDtypeStruct(dual_wave.shape, BF16),
            ),
            in_specs=[vmem, hbm, hbm, smem, hbm, hbm, smem, hbm, smem, smem],
            out_specs=(vmem, vmem, vmem),
            scratch_shapes=[
                V(dual_wave.shape, BF16),
                V(blocks.shape, BF16),
                V(thresholds.shape, F32),
                V(seen.shape, F32),
                V(dual_data.shape, F32),
                V((NB, 2 * L, L), BF16),
                V((NB, 2 * L, 2 * L), BF16),
                V((NB * R, 3 * R), BF16),
                V((4 * R, NB * R), BF16),
                V((NB * R, C * L + L), BF16),
                V((NB, C, R, 2 * L), BF16),
                V((ITERS, 3, R, C * L), BF16),
                V((8, 128), BF16),
                V((ITERS, 3 * T1, C, PIX), BF16),
                V((ITERS, 2, 3, R, L), BF16),
                V((ITERS, R, L), BF16),
                V((ITERS, R, C * L), BF16),
                V((ITERS, 2, R, C * L), BF16),
                V((ITERS, 2, R, L), BF16),
                V((ITERS, 2, 3, R, L), BF16),
                V((ITERS, 2, T1, C, PIX), BF16),
                V((ITERS, 2, T1, C, PIX), BF16),
                V((KB + 1, C, max(PIX, VB)), F32),
                V(dual_wave.shape, BF16),
                V(image.shape, F32),
                V((R, C * L), F32),
                V((RB, C, VB), BF16),
                pltpu.SMEM((4, max(KB, 3 * T1)), jnp.int32),
                pltpu.SemaphoreType.DMA((5,)),
                pltpu.SemaphoreType.DMA((messages,)),
                pltpu.SemaphoreType.DMA((messages,)),
            ],
            compiler_params=pltpu.CompilerParams(collective_id=0, has_side_effects=True, vmem_limit_bytes=60 << 20),
        )(image, dual_wave, thresholds, taps, seen, dual_data, radius, blocks, row_ids, col_ids)

    dev = P("facet", "grp")
    rows = P(None, "facet", "grp")
    wave = P(None, None, "facet", "grp")
    return jax.shard_map(
        per_device,
        mesh=mesh,
        in_specs=(rows, wave, rows, P(), dev, dev, dev, dev, dev, dev),
        out_specs=(rows, dev, wave),
        check_vma=False,
    )
```

```python
import functools

import jax
import jax.numpy as jnp
from jax import lax
from jax.experimental import pallas as pl
from jax.experimental.pallas import tpu as pltpu
from jax.sharding import PartitionSpec as P

W = 3
TS = 16
ITERS = 2
MESH = pl.DeviceIdType.MESH
F32 = jnp.float32
BF16 = jnp.bfloat16
ROWS = ((-1, 0), (1, 0))
SIDES = ((0, -1), (0, 1), (-1, -1), (-1, 1), (1, -1), (1, 1))
DIRS = ROWS + SIDES
ROW_SLOT = {0: 0, 1: 1, -1: 2}
SIDE_SLOT = {1: 0, -1: 1}


def iota(shape, dim):
    return lax.broadcasted_iota(jnp.int32, shape, dim)


def tap_matrix(position, taps):
    out = jnp.zeros(position.shape, F32)
    for tap, value in enumerate(taps):
        out = jnp.where(position == tap, value, out)
    return out


def swap_groups(items):
    count = len(items)
    lanes = items[0].shape[-1]
    group = iota(items[0].shape, 1) // TS
    step = count // 2
    while step:
        low = (group // step) % 2 == 0
        out = list(items)
        for a in range(count):
            if (a // step) % 2 == 0:
                first, second = items[a], items[a + step]
                out[a] = jnp.where(low, first, pltpu.roll(second, step * TS, 1))
                out[a + step] = jnp.where(low, pltpu.roll(first, lanes - step * TS, 1), second)
        items = out
        step //= 2
    return items


def kernel(
    sizes,
    image_hbm, dual_wave, thresholds, taps, seen, dual_data, radius, blocks, row_ids, col_ids,
    image_out, data_out, wave_out,
    image, u_in, ops, thr, vis, vdat, ttap, stap, rtap, ptap, ycols, rfilt,
    near, zrim, ztile, zedge, zedge_own, rim_own, rim, edge_own, edge, tsum_own, tsum,
    parts, uslot, vslot, xslot, turn, links,
    local_sem, send_sem, recv_sem,
):
    nf, ng, NB, C, R, L, KB, RB, PIX, VB, TAPS, NT3 = sizes
    f = lax.axis_index("facet")
    g = lax.axis_index("grp")
    T1 = L // TS
    LC = C * L
    EW = L // C

    def exists(d):
        df, dg = d
        ok = None
        for test in ([f > 0] if df < 0 else [f < nf - 1] if df > 0 else []) + (
            [g > 0] if dg < 0 else [g < ng - 1] if dg > 0 else []
        ):
            ok = test if ok is None else jnp.logical_and(ok, test)
        return ok

    def back(d):
        return (-d[0], -d[1])

    def where_to(d):
        return {"facet": f + d[0], "grp": g + d[1]}

    loads = [
        pltpu.make_async_copy(src, dst, local_sem.at[n])
        for n, (src, dst) in enumerate(
            ((dual_wave, u_in), (dual_data, vdat), (blocks, ops), (seen, vis), (thresholds, thr), (image_hbm, image))
        )
    ]
    for load in loads:
        load.start()

    for ref in (rim, edge, tsum, near, zedge):
        ref[...] = jnp.zeros(ref.shape, ref.dtype)
    for it in range(ITERS):
        ztile[it, :T1] = jnp.zeros((T1, C, PIX), BF16)
        ztile[it, 2 * T1 :] = jnp.zeros((T1, C, PIX), BF16)

    barrier = pltpu.get_barrier_semaphore()
    for d in DIRS:
        @pl.when(exists(d))
        def _(d=d):
            pl.semaphore_signal(barrier, inc=1, device_id=where_to(d), device_id_type=MESH)

    src = iota((L, L), 0)
    dst = iota((L, L), 1)
    m_dst = dst % EW
    m_src = src % EW
    row_out = iota((2 * R, NB * R), 0)
    row_out = jnp.where(row_out < R, row_out, jnp.where(row_out < R + W, row_out - R - W, jnp.where(row_out < R + 2 * W, row_out - W, 4 * L)))
    row_in = iota((2 * R, NB * R), 1)
    row_at = iota((R, 3 * R), 1)
    row_at = jnp.where(row_at < R, row_at, jnp.where(row_at < 2 * R, row_at - 2 * R, row_at - R))
    row_to = iota((R, 3 * R), 0)
    synth_rows = jnp.zeros((2 * R, NB * R), F32)
    sub, lane = iota((EW, L), 0), iota((EW, L), 1)
    last_sub = sub + L - EW
    m_lane = lane % EW
    over_col = jnp.where(m_lane < W, m_lane - W, jnp.where(m_lane < 2 * W, L + m_lane - W, 4 * L))
    halo_col = jnp.where(sub < W, L + sub, jnp.where(sub < 2 * W, sub - 2 * W, 4 * L))
    none = jnp.zeros((EW, L), F32)

    def band(values, sign):
        ahead = (sign * (lane - sub) + W + L) % L
        base = tap_matrix(ahead, values)
        pieces = [base] + [pltpu.roll(base, n * EW, 1) for n in range(1, C)]
        pieces[0] = jnp.where(lane < L // 2, base, 0.0)
        pieces[-1] = jnp.where(lane < L // 2, 0.0, pieces[-1])
        return pieces

    def store(ref, b, row, col, pieces, low=False):
        for n in range(0, len(pieces), 2):
            value = jnp.concatenate(pieces[n : n + 2], axis=0)
            high = value.astype(BF16)
            ref[b, row + n * EW : row + (n + 2) * EW, col : col + L] = high
            if low:
                rest = (value - high.astype(F32)).astype(BF16)
                ref[b, row + L + n * EW : row + L + (n + 2) * EW, col : col + L] = rest

    for b in range(NB):
        rt = [taps[t, 0, b] for t in range(TAPS)]
        ct = [taps[t, 1, b] for t in range(TAPS)]
        ch = [0.5 * t for t in ct]
        store(stap, b, 0, 0, band(ct, 1), True)
        rim_first = tap_matrix(over_col + W - sub, ct)
        rim_last = tap_matrix(over_col + W - last_sub, ct)
        store(stap, b, 0, L, [rim_first] + [none] * (C - 2) + [rim_last], True)
        store(ttap, b, 0, 0, band(ch, -1))
        store(ttap, b, L, 0, [tap_matrix(halo_col - lane + W, ch)] * C)
        rtap[b * R : (b + 1) * R] = tap_matrix(row_at - row_to + W, rt).astype(BF16)
        synth_rows = jnp.where(row_in // R == b, tap_matrix(row_out + W - (row_in - b * R), rt), synth_rows)
    rows_high = synth_rows.astype(BF16)
    ptap[: 2 * R] = rows_high
    ptap[2 * R :] = (synth_rows - rows_high.astype(F32)).astype(BF16)
    for side, (ids, count) in enumerate(((col_ids, NT3), (row_ids, RB))):
        for k in range(KB):
            before = KB
            for j in range(k):
                before = jnp.where(ids[0, 0, j] == ids[0, 0, k], j, before)
            links[2 * side, k] = before
        for q in range(count):
            last = KB
            for k in range(KB):
                last = jnp.where(ids[0, 0, k] == q, k, last)
            links[2 * side + 1, q] = last
    parts[KB] = jnp.zeros(parts.shape[1:], F32)
    pick = jnp.where(jnp.logical_or(jnp.logical_and(m_dst < W, src == m_dst), jnp.logical_and(jnp.logical_and(m_dst >= W, m_dst < 2 * W), src == L - 2 * W + m_dst)), 1.0, 0.0).astype(BF16)
    place = jnp.where(jnp.logical_or(jnp.logical_and(m_src < W, dst == L - W + m_src), jnp.logical_and(jnp.logical_and(m_src >= W, m_src < 2 * W), dst == m_src - W)), 1.0, 0.0).astype(BF16)
    q_to = iota((R, 2 * R), 0)
    q_at = iota((R, 2 * R), 1)
    settle = jnp.where(jnp.logical_or(jnp.logical_and(q_to < W, q_at == q_to + W), jnp.logical_and(q_to >= R - W, q_at == q_to + W)), 1.0, 0.0).astype(BF16)
    lane_c = iota((R, L), 1) // EW
    lane_m = iota((R, L), 1) % EW

    def dot(a, b):
        return jnp.dot(a, b, preferred_element_type=F32)

    tall = 3 - (f == 0).astype(jnp.int32) - (f == nf - 1).astype(jnp.int32)
    wide = 3 - (g == 0).astype(jnp.int32) - (g == ng - 1).astype(jnp.int32)
    pl.semaphore_wait(barrier, tall * wide - 1)

    sent = []

    def message(it, kind, d, src_ref, dst_ref):
        slot = (it * 4 + kind) * 8 + DIRS.index(d)
        return pltpu.make_async_remote_copy(
            src_ref=src_ref, dst_ref=dst_ref, send_sem=send_sem.at[slot], recv_sem=recv_sem.at[slot],
            device_id=where_to(d), device_id_type=MESH,
        )

    def send(copies):
        for d, copy in copies:
            pl.when(exists(d))(copy.start)
        sent.extend(copies)

    def receive(copies):
        for d, copy in copies:
            pl.when(exists(back(d)))(copy.wait_recv)

    loads[0].wait()
    for it in range(ITERS):
        for b in range(NB):
            cells = (u_in[b] if it == 0 else uslot[b]).reshape(C * R, L)
            cols = dot(jnp.concatenate([cells, cells], axis=1), stap[b])
            rimc = jnp.zeros((R, L), F32)
            for c in range(C):
                part = cols[c * R : (c + 1) * R]
                ycols[b * R : (b + 1) * R, c * L : (c + 1) * L] = part[:, :L].astype(BF16)
                rimc = jnp.where(lane_c == c, part[:, L:], rimc)
            ycols[b * R : (b + 1) * R, LC:] = rimc.astype(BF16)
        smooth = dot(ptap[...], ycols[...])
        smooth = smooth[: 2 * R] + smooth[2 * R :]
        rim_own[it] = smooth[R:, :LC].astype(BF16)
        edge_own[it] = smooth[:, LC:].astype(BF16).reshape(2, R, L)
        xslot[...] = smooth[:R, :LC]
        msg_a = [(d, message(it, 0, d, rim_own.at[it], rim.at[it, ROW_SLOT[d[0]] - 1])) for d in ROWS]
        msg_a += [
            (d, message(it, 0, d, edge_own.at[it, 0 if d[0] == 0 else 1], edge.at[it, SIDE_SLOT[d[1]], ROW_SLOT[d[0]]]))
            for d in SIDES
        ]
        send(msg_a)

        if it == 0:
            loads[1].wait()
            for r in range(RB):
                turn[r] = vdat[0, 0, r].astype(BF16)
            loads[2].wait()
        for k in range(KB):
            part = lax.dot_general(
                turn[row_ids[0, 0, k]], ops[0, 0, k], (((1,), (1,)), ((), ())), preferred_element_type=F32
            )
            parts[k] = part + parts[links[0, k]] if k else part

        def tile_total(q):
            return parts[links[1, q]]

        for t in range(T1):
            tsum_own[it, 0, t] = tile_total(t).astype(BF16)
            tsum_own[it, 1, t] = tile_total(2 * T1 + t).astype(BF16)
        msg_b = [
            (d, message(it, 1, d, tsum_own.at[it, 0 if d[0] < 0 else 1], tsum.at[it, ROW_SLOT[d[0]] - 1])) for d in ROWS
        ]
        send(msg_b)
        totals = [tile_total(T1 + t) for t in range(T1)]

        receive(msg_a)
        rows_in = dot(settle, rim[it].reshape(2 * R, LC))
        came = [jnp.where(lane_m >= W, edge[it, 0, s].astype(F32), edge[it, 1, s].astype(F32)) for s in range(3)]
        corner = dot(settle, jnp.concatenate([came[1], came[2]], axis=0).astype(BF16))
        side = came[0] + corner
        spread = jnp.concatenate([jnp.where(lane_c == c, side, 0.0) for c in range(C)], axis=0).astype(BF16)
        side_in = dot(spread, place)
        receive(msg_b)
        totals = [totals[t] + (tsum[it, 0, t].astype(F32) + tsum[it, 1, t].astype(F32)) for t in range(T1)]
        lines = []
        for h in range(PIX // L):
            lines += swap_groups([t[:, h * L : (h + 1) * L] for t in totals])
        backward = jnp.swapaxes(jnp.stack(lines), 0, 1)

        if it == 0:
            loads[5].wait()
        extrap = []
        for c in range(C):
            here = slice(c * L, (c + 1) * L)
            old = image[c] if it == 0 else vslot[c]
            grad = backward[c] + (xslot[:, here] + rows_in[:, here] + side_in[c * R : (c + 1) * R])
            new = jnp.maximum(old - 0.5 * grad, 0.0)
            if it == ITERS - 1:
                image_out[c] = new
            else:
                vslot[c] = new
            ext = (2.0 * new - old).astype(BF16)
            near[it, 0, :, here] = ext
            extrap.append(ext)
        msg_c = [(d, message(it, 2, d, near.at[it, 0], near.at[it, ROW_SLOT[d[0]]])) for d in ROWS]
        flat = jnp.concatenate(extrap, axis=0)
        edges = dot(flat, pick)
        mine = jnp.zeros((R, L), F32)
        for c in range(C):
            mine = jnp.where(lane_c == c, edges[c * R : (c + 1) * R], mine)
        zedge_own[it] = mine.astype(BF16)
        msg_c += [
            (d, message(it, 2, d, zedge_own.at[it], zedge.at[it, SIDE_SLOT[d[1]], ROW_SLOT[d[0]]])) for d in SIDES
        ]
        send(msg_c)
        turned = jnp.swapaxes(flat.astype(F32).reshape(C, R, L), 0, 1)
        for h in range(PIX // L):
            tiles = swap_groups([turned[h * T1 + i] for i in range(T1)])
            for t in range(T1):
                ztile[it, T1 + t, :, h * L : (h + 1) * L] = tiles[t].astype(BF16)
        own_tiles = ztile.at[it, pl.ds(T1, T1)]
        msg_d = [
            (d, message(it, 3, d, own_tiles, ztile.at[it, pl.ds(2 * T1 if d[0] < 0 else 0, T1)])) for d in ROWS
        ]
        send(msg_d)

        receive(msg_c)
        zside = [jnp.where(lane_m >= W, zedge[it, 0, s].astype(F32), zedge[it, 1, s].astype(F32)) for s in range(3)]
        zside = jnp.concatenate(zside, axis=0).astype(BF16)
        side_rows = dot(rtap[...], zside)
        for c in range(C):
            lines_c = dot(rtap[...], near[it, :, :, c * L : (c + 1) * L].reshape(3 * R, L)).astype(BF16)
            side_c = jnp.where(iota((NB * R, L), 1) // EW == c, side_rows, 0.0).astype(BF16)
            rfilt[:, c, :, :L] = lines_c.reshape(NB, R, L)
            rfilt[:, c, :, L:] = side_c.reshape(NB, R, L)
        if it == 0:
            loads[4].wait()
        for b in range(NB):
            half = dot(rfilt[b].reshape(C * R, 2 * L), ttap[b]).reshape(C, R, L)
            cells = (u_in[b] if it == 0 else uslot[b]).astype(F32)
            widened = cells + half
            magnitude = jnp.sqrt(jnp.sum(widened * widened, axis=0))
            bound = thr[b]
            shrink = bound / jnp.maximum(magnitude, bound)
            new_u = (widened * shrink[None]).astype(BF16)
            if it == ITERS - 1:
                wave_out[b] = new_u
            else:
                uslot[b] = new_u

        receive(msg_d)
        for k in range(KB):
            part = dot(ztile[it, col_ids[0, 0, k]], ops[0, 0, k])
            parts[k] = part + parts[links[2, k]] if k else part
        if it == 0:
            loads[3].wait()
        for r in range(RB):
            pred = parts[links[3, r]]
            moved = (vdat[0, 0, r] if it == 0 else data_out[0, 0, r]) + 0.5 * pred
            offset = 2.0 * moved - vis[0, 0, r]
            length = jnp.sqrt(jnp.sum(jnp.sum(offset * offset, axis=0, keepdims=True), axis=1, keepdims=True))
            ball = radius[0, 0, r]
            nearest = vis[0, 0, r] + offset * (ball / jnp.maximum(length, ball))
            new_v = moved - 0.5 * nearest
            data_out[0, 0, r] = new_v
            turn[r] = new_v.astype(BF16)

    for d, copy in sent:
        pl.when(exists(d))(copy.wait_send)


def hand_over(*refs):
    count = (len(refs) - 2) // 3
    sources, results, held = (refs[n * count : (n + 1) * count] for n in range(3))
    in_sem, out_sem = refs[-2:]
    into = [pltpu.make_async_copy(sources[n], held[n], in_sem.at[n]) for n in range(count)]
    out = [pltpu.make_async_copy(held[n], results[n], out_sem.at[n]) for n in range(count)]
    for copy in into:
        copy.start()
    for n in range(count):
        into[n].wait()
        out[n].start()
    for copy in out:
        copy.wait()


def passed_on(arrays):
    any_spec = pl.BlockSpec(memory_space=pl.ANY)
    return pl.pallas_call(
        hand_over,
        out_shape=tuple(jax.ShapeDtypeStruct(a.shape, a.dtype) for a in arrays),
        in_specs=[any_spec] * len(arrays),
        out_specs=(any_spec,) * len(arrays),
        scratch_shapes=[pltpu.VMEM(a.shape, a.dtype) for a in arrays]
        + [pltpu.SemaphoreType.DMA((len(arrays),))] * 2,
        compiler_params=pltpu.CompilerParams(vmem_limit_bytes=62 << 20),
    )(*arrays)


def solution(mesh):
    nf, ng = mesh.shape["facet"], mesh.shape["grp"]

    def per_device(image, dual_wave, thresholds, taps, seen, dual_data, radius, blocks, row_ids, col_ids):
        taps = jnp.transpose(taps, (2, 1, 0))
        C, R, L = image.shape
        TAPS, _, NB = taps.shape
        KB, PIX, VB = blocks.shape[2:]
        RB = seen.shape[2]
        T1 = L // TS
        sizes = (nf, ng, NB, C, R, L, KB, RB, PIX, VB, TAPS, 3 * T1)
        vmem = pl.BlockSpec(memory_space=pltpu.VMEM)
        smem = pl.BlockSpec(memory_space=pltpu.SMEM)
        hbm = pl.BlockSpec(memory_space=pltpu.HBM)
        V = pltpu.VMEM
        messages = ITERS * 4 * 8
        results = pl.pallas_call(
            functools.partial(kernel, sizes),
            out_shape=(
                jax.ShapeDtypeStruct(image.shape, F32),
                jax.ShapeDtypeStruct(dual_data.shape, F32),
                jax.ShapeDtypeStruct(dual_wave.shape, BF16),
            ),
            in_specs=[hbm, hbm, hbm, smem, hbm, hbm, smem, hbm, smem, smem],
            out_specs=(vmem, vmem, vmem),
            scratch_shapes=[
                V(image.shape, F32),
                V(dual_wave.shape, BF16),
                V(blocks.shape, BF16),
                V(thresholds.shape, F32),
                V(seen.shape, F32),
                V(dual_data.shape, F32),
                V((NB, 2 * L, L), BF16),
                V((NB, 2 * L, 2 * L), BF16),
                V((NB * R, 3 * R), BF16),
                V((4 * R, NB * R), BF16),
                V((NB * R, C * L + L), BF16),
                V((NB, C, R, 2 * L), BF16),
                V((ITERS, 3, R, C * L), BF16),
                V((8, 128), BF16),
                V((ITERS, 3 * T1, C, PIX), BF16),
                V((ITERS, 2, 3, R, L), BF16),
                V((ITERS, R, L), BF16),
                V((ITERS, R, C * L), BF16),
                V((ITERS, 2, R, C * L), BF16),
                V((ITERS, 2, R, L), BF16),
                V((ITERS, 2, 3, R, L), BF16),
                V((ITERS, 2, T1, C, PIX), BF16),
                V((ITERS, 2, T1, C, PIX), BF16),
                V((KB + 1, C, max(PIX, VB)), F32),
                V(dual_wave.shape, BF16),
                V(image.shape, F32),
                V((R, C * L), F32),
                V((RB, C, VB), BF16),
                pltpu.SMEM((4, max(KB, 3 * T1)), jnp.int32),
                pltpu.SemaphoreType.DMA((6,)),
                pltpu.SemaphoreType.DMA((messages,)),
                pltpu.SemaphoreType.DMA((messages,)),
            ],
            compiler_params=pltpu.CompilerParams(collective_id=0, has_side_effects=True, vmem_limit_bytes=60 << 20),
        )(image, dual_wave, thresholds, taps, seen, dual_data, radius, blocks, row_ids, col_ids)
        return passed_on(results)

    dev = P("facet", "grp")
    rows = P(None, "facet", "grp")
    wave = P(None, None, "facet", "grp")
    return jax.shard_map(
        per_device,
        mesh=mesh,
        in_specs=(rows, wave, rows, P(), dev, dev, dev, dev, dev, dev),
        out_specs=(rows, dev, wave),
        check_vma=False,
    )
```

```python
import functools

import jax
import jax.numpy as jnp
from jax import lax
from jax.experimental import pallas as pl
from jax.experimental.pallas import tpu as pltpu
from jax.sharding import PartitionSpec as P

W = 3
TS = 16
ITERS = 2
MESH = pl.DeviceIdType.MESH
F32 = jnp.float32
BF16 = jnp.bfloat16
ROWS = ((-1, 0), (1, 0))
SIDES = ((0, -1), (0, 1), (-1, -1), (-1, 1), (1, -1), (1, 1))
DIRS = ROWS + SIDES
ROW_SLOT = {0: 0, 1: 1, -1: 2}
SIDE_SLOT = {1: 0, -1: 1}


def iota(shape, dim):
    return lax.broadcasted_iota(jnp.int32, shape, dim)


def tap_matrix(position, taps):
    out = jnp.zeros(position.shape, F32)
    for tap, value in enumerate(taps):
        out = jnp.where(position == tap, value, out)
    return out


def swap_groups(items):
    count = len(items)
    lanes = items[0].shape[-1]
    group = iota(items[0].shape, 1) // TS
    step = count // 2
    while step:
        low = (group // step) % 2 == 0
        out = list(items)
        for a in range(count):
            if (a // step) % 2 == 0:
                first, second = items[a], items[a + step]
                out[a] = jnp.where(low, first, pltpu.roll(second, step * TS, 1))
                out[a + step] = jnp.where(low, pltpu.roll(first, lanes - step * TS, 1), second)
        items = out
        step //= 2
    return items


def kernel(
    sizes,
    image_hbm, dual_wave, thresholds, taps, seen, dual_data, radius, blocks, row_ids, col_ids,
    image_out, data_out, wave_out,
    image, u_in, ops, thr, vis, vdat, ttap, stap, rtap, ptap, ycols, rfilt,
    near, zrim, ztile, zedge, zedge_own, rim_own, rim, edge_own, edge, tsum_own, tsum,
    parts, uslot, vslot, xslot, turn, links,
    local_sem, send_sem, recv_sem,
):
    nf, ng, NB, C, R, L, KB, RB, PIX, VB, TAPS, NT3 = sizes
    f = lax.axis_index("facet")
    g = lax.axis_index("grp")
    T1 = L // TS
    LC = C * L
    EW = L // C

    def exists(d):
        df, dg = d
        ok = None
        for test in ([f > 0] if df < 0 else [f < nf - 1] if df > 0 else []) + (
            [g > 0] if dg < 0 else [g < ng - 1] if dg > 0 else []
        ):
            ok = test if ok is None else jnp.logical_and(ok, test)
        return ok

    def back(d):
        return (-d[0], -d[1])

    def where_to(d):
        return {"facet": f + d[0], "grp": g + d[1]}

    loads = [
        pltpu.make_async_copy(src, dst, local_sem.at[n])
        for n, (src, dst) in enumerate(
            ((dual_wave, u_in), (dual_data, vdat), (blocks, ops), (seen, vis), (thresholds, thr), (image_hbm, image))
        )
    ]
    for load in loads:
        load.start()

    for ref in (rim, edge, tsum, near, zedge):
        ref[...] = jnp.zeros(ref.shape, ref.dtype)
    for it in range(ITERS):
        ztile[it, :T1] = jnp.zeros((T1, C, PIX), BF16)
        ztile[it, 2 * T1 :] = jnp.zeros((T1, C, PIX), BF16)

    barrier = pltpu.get_barrier_semaphore()
    for d in DIRS:
        @pl.when(exists(d))
        def _(d=d):
            pl.semaphore_signal(barrier, inc=1, device_id=where_to(d), device_id_type=MESH)

    src = iota((L, L), 0)
    dst = iota((L, L), 1)
    m_dst = dst % EW
    m_src = src % EW
    row_out = iota((2 * R, NB * R), 0)
    row_out = jnp.where(row_out < R, row_out, jnp.where(row_out < R + W, row_out - R - W, jnp.where(row_out < R + 2 * W, row_out - W, 4 * L)))
    row_in = iota((2 * R, NB * R), 1)
    row_at = iota((R, 3 * R), 1)
    row_at = jnp.where(row_at < R, row_at, jnp.where(row_at < 2 * R, row_at - 2 * R, row_at - R))
    row_to = iota((R, 3 * R), 0)
    synth_rows = jnp.zeros((2 * R, NB * R), F32)
    sub, lane = iota((EW, L), 0), iota((EW, L), 1)
    last_sub = sub + L - EW
    m_lane = lane % EW
    over_col = jnp.where(m_lane < W, m_lane - W, jnp.where(m_lane < 2 * W, L + m_lane - W, 4 * L))
    halo_col = jnp.where(sub < W, L + sub, jnp.where(sub < 2 * W, sub - 2 * W, 4 * L))
    none = jnp.zeros((EW, L), F32)

    def band(values, sign):
        ahead = (sign * (lane - sub) + W + L) % L
        base = tap_matrix(ahead, values)
        pieces = [base] + [pltpu.roll(base, n * EW, 1) for n in range(1, C)]
        pieces[0] = jnp.where(lane < L // 2, base, 0.0)
        pieces[-1] = jnp.where(lane < L // 2, 0.0, pieces[-1])
        return pieces

    def store(ref, b, row, col, pieces, low=False):
        for n in range(0, len(pieces), 2):
            value = jnp.concatenate(pieces[n : n + 2], axis=0)
            high = value.astype(BF16)
            ref[b, row + n * EW : row + (n + 2) * EW, col : col + L] = high
            if low:
                rest = (value - high.astype(F32)).astype(BF16)
                ref[b, row + L + n * EW : row + L + (n + 2) * EW, col : col + L] = rest

    for b in range(NB):
        rt = [taps[t, 0, b] for t in range(TAPS)]
        ct = [taps[t, 1, b] for t in range(TAPS)]
        ch = [0.5 * t for t in ct]
        store(stap, b, 0, 0, band(ct, 1), True)
        rim_first = tap_matrix(over_col + W - sub, ct)
        rim_last = tap_matrix(over_col + W - last_sub, ct)
        store(stap, b, 0, L, [rim_first] + [none] * (C - 2) + [rim_last], True)
        store(ttap, b, 0, 0, band(ch, -1))
        store(ttap, b, L, 0, [tap_matrix(halo_col - lane + W, ch)] * C)
        rtap[b * R : (b + 1) * R] = tap_matrix(row_at - row_to + W, rt).astype(BF16)
        synth_rows = jnp.where(row_in // R == b, tap_matrix(row_out + W - (row_in - b * R), rt), synth_rows)
    rows_high = synth_rows.astype(BF16)
    ptap[: 2 * R] = rows_high
    ptap[2 * R :] = (synth_rows - rows_high.astype(F32)).astype(BF16)
    for side, (ids, count) in enumerate(((col_ids, NT3), (row_ids, RB))):
        for k in range(KB):
            before = KB
            for j in range(k):
                before = jnp.where(ids[0, 0, j] == ids[0, 0, k], j, before)
            links[2 * side, k] = before
        for q in range(count):
            last = KB
            for k in range(KB):
                last = jnp.where(ids[0, 0, k] == q, k, last)
            links[2 * side + 1, q] = last
    parts[KB] = jnp.zeros(parts.shape[1:], F32)
    pick = jnp.where(jnp.logical_or(jnp.logical_and(m_dst < W, src == m_dst), jnp.logical_and(jnp.logical_and(m_dst >= W, m_dst < 2 * W), src == L - 2 * W + m_dst)), 1.0, 0.0).astype(BF16)
    place = jnp.where(jnp.logical_or(jnp.logical_and(m_src < W, dst == L - W + m_src), jnp.logical_and(jnp.logical_and(m_src >= W, m_src < 2 * W), dst == m_src - W)), 1.0, 0.0).astype(BF16)
    q_to = iota((R, 2 * R), 0)
    q_at = iota((R, 2 * R), 1)
    settle = jnp.where(jnp.logical_or(jnp.logical_and(q_to < W, q_at == q_to + W), jnp.logical_and(q_to >= R - W, q_at == q_to + W)), 1.0, 0.0).astype(BF16)
    lane_c = iota((R, L), 1) // EW
    lane_m = iota((R, L), 1) % EW

    def dot(a, b):
        return jnp.dot(a, b, preferred_element_type=F32)

    tall = 3 - (f == 0).astype(jnp.int32) - (f == nf - 1).astype(jnp.int32)
    wide = 3 - (g == 0).astype(jnp.int32) - (g == ng - 1).astype(jnp.int32)
    pl.semaphore_wait(barrier, tall * wide - 1)

    sent = []

    def message(it, kind, d, src_ref, dst_ref):
        slot = (it * 4 + kind) * 8 + DIRS.index(d)
        return pltpu.make_async_remote_copy(
            src_ref=src_ref, dst_ref=dst_ref, send_sem=send_sem.at[slot], recv_sem=recv_sem.at[slot],
            device_id=where_to(d), device_id_type=MESH,
        )

    def send(copies):
        for d, copy in copies:
            pl.when(exists(d))(copy.start)
        sent.extend(copies)

    def receive(copies):
        for d, copy in copies:
            pl.when(exists(back(d)))(copy.wait_recv)

    for it in range(ITERS):
        if it == 0:
            loads[1].wait()
            for r in range(RB):
                turn[r] = vdat[0, 0, r].astype(BF16)
            loads[2].wait()
        for k in range(KB):
            part = lax.dot_general(
                turn[row_ids[0, 0, k]], ops[0, 0, k], (((1,), (1,)), ((), ())), preferred_element_type=F32
            )
            parts[k] = part + parts[links[0, k]] if k else part

        def tile_total(q):
            return parts[links[1, q]]

        for t in range(T1):
            tsum_own[it, 0, t] = tile_total(t).astype(BF16)
            tsum_own[it, 1, t] = tile_total(2 * T1 + t).astype(BF16)
        msg_b = [
            (d, message(it, 1, d, tsum_own.at[it, 0 if d[0] < 0 else 1], tsum.at[it, ROW_SLOT[d[0]] - 1])) for d in ROWS
        ]
        send(msg_b)
        totals = [tile_total(T1 + t) for t in range(T1)]

        if it == 0:
            loads[0].wait()
        for b in range(NB):
            cells = (u_in[b] if it == 0 else uslot[b]).reshape(C * R, L)
            cols = dot(jnp.concatenate([cells, cells], axis=1), stap[b])
            rimc = jnp.zeros((R, L), F32)
            for c in range(C):
                part = cols[c * R : (c + 1) * R]
                ycols[b * R : (b + 1) * R, c * L : (c + 1) * L] = part[:, :L].astype(BF16)
                rimc = jnp.where(lane_c == c, part[:, L:], rimc)
            ycols[b * R : (b + 1) * R, LC:] = rimc.astype(BF16)
        smooth = dot(ptap[...], ycols[...])
        smooth = smooth[: 2 * R] + smooth[2 * R :]
        rim_own[it] = smooth[R:, :LC].astype(BF16)
        edge_own[it] = smooth[:, LC:].astype(BF16).reshape(2, R, L)
        xslot[...] = smooth[:R, :LC]
        msg_a = [(d, message(it, 0, d, rim_own.at[it], rim.at[it, ROW_SLOT[d[0]] - 1])) for d in ROWS]
        msg_a += [
            (d, message(it, 0, d, edge_own.at[it, 0 if d[0] == 0 else 1], edge.at[it, SIDE_SLOT[d[1]], ROW_SLOT[d[0]]]))
            for d in SIDES
        ]
        send(msg_a)

        receive(msg_b)
        totals = [totals[t] + (tsum[it, 0, t].astype(F32) + tsum[it, 1, t].astype(F32)) for t in range(T1)]
        lines = []
        for h in range(PIX // L):
            lines += swap_groups([t[:, h * L : (h + 1) * L] for t in totals])
        backward = jnp.swapaxes(jnp.stack(lines), 0, 1)

        receive(msg_a)
        rows_in = dot(settle, rim[it].reshape(2 * R, LC))
        came = [jnp.where(lane_m >= W, edge[it, 0, s].astype(F32), edge[it, 1, s].astype(F32)) for s in range(3)]
        corner = dot(settle, jnp.concatenate([came[1], came[2]], axis=0).astype(BF16))
        side = came[0] + corner
        spread = jnp.concatenate([jnp.where(lane_c == c, side, 0.0) for c in range(C)], axis=0).astype(BF16)
        side_in = dot(spread, place)
        if it == 0:
            loads[5].wait()
        extrap = []
        for c in range(C):
            here = slice(c * L, (c + 1) * L)
            old = image[c] if it == 0 else vslot[c]
            grad = backward[c] + (xslot[:, here] + rows_in[:, here] + side_in[c * R : (c + 1) * R])
            new = jnp.maximum(old - 0.5 * grad, 0.0)
            if it == ITERS - 1:
                image_out[c] = new
            else:
                vslot[c] = new
            ext = (2.0 * new - old).astype(BF16)
            near[it, 0, :, here] = ext
            extrap.append(ext)
        msg_c = [(d, message(it, 2, d, near.at[it, 0], near.at[it, ROW_SLOT[d[0]]])) for d in ROWS]
        send(msg_c)
        flat = jnp.concatenate(extrap, axis=0)
        edges = dot(flat, pick)
        mine = jnp.zeros((R, L), F32)
        for c in range(C):
            mine = jnp.where(lane_c == c, edges[c * R : (c + 1) * R], mine)
        zedge_own[it] = mine.astype(BF16)
        msg_e = [
            (d, message(it, 2, d, zedge_own.at[it], zedge.at[it, SIDE_SLOT[d[1]], ROW_SLOT[d[0]]])) for d in SIDES
        ]
        send(msg_e)
        turned = jnp.swapaxes(flat.astype(F32).reshape(C, R, L), 0, 1)
        for h in range(PIX // L):
            tiles = swap_groups([turned[h * T1 + i] for i in range(T1)])
            for t in range(T1):
                ztile[it, T1 + t, :, h * L : (h + 1) * L] = tiles[t].astype(BF16)
        own_tiles = ztile.at[it, pl.ds(T1, T1)]
        msg_d = [
            (d, message(it, 3, d, own_tiles, ztile.at[it, pl.ds(2 * T1 if d[0] < 0 else 0, T1)])) for d in ROWS
        ]
        send(msg_d)

        receive(msg_c)
        receive(msg_e)
        zside = [jnp.where(lane_m >= W, zedge[it, 0, s].astype(F32), zedge[it, 1, s].astype(F32)) for s in range(3)]
        zside = jnp.concatenate(zside, axis=0).astype(BF16)
        side_rows = dot(rtap[...], zside)
        for c in range(C):
            lines_c = dot(rtap[...], near[it, :, :, c * L : (c + 1) * L].reshape(3 * R, L)).astype(BF16)
            side_c = jnp.where(iota((NB * R, L), 1) // EW == c, side_rows, 0.0).astype(BF16)
            rfilt[:, c, :, :L] = lines_c.reshape(NB, R, L)
            rfilt[:, c, :, L:] = side_c.reshape(NB, R, L)
        if it == 0:
            loads[4].wait()
        for b in range(NB):
            half = dot(rfilt[b].reshape(C * R, 2 * L), ttap[b]).reshape(C, R, L)
            cells = (u_in[b] if it == 0 else uslot[b]).astype(F32)
            widened = cells + half
            magnitude = jnp.sqrt(jnp.sum(widened * widened, axis=0))
            bound = thr[b]
            shrink = bound / jnp.maximum(magnitude, bound)
            new_u = (widened * shrink[None]).astype(BF16)
            if it == ITERS - 1:
                wave_out[b] = new_u
            else:
                uslot[b] = new_u

        receive(msg_d)
        for k in range(KB):
            part = dot(ztile[it, col_ids[0, 0, k]], ops[0, 0, k])
            parts[k] = part + parts[links[2, k]] if k else part
        if it == 0:
            loads[3].wait()
        for r in range(RB):
            pred = parts[links[3, r]]
            moved = (vdat[0, 0, r] if it == 0 else data_out[0, 0, r]) + 0.5 * pred
            offset = 2.0 * moved - vis[0, 0, r]
            length = jnp.sqrt(jnp.sum(jnp.sum(offset * offset, axis=0, keepdims=True), axis=1, keepdims=True))
            ball = radius[0, 0, r]
            nearest = vis[0, 0, r] + offset * (ball / jnp.maximum(length, ball))
            new_v = moved - 0.5 * nearest
            data_out[0, 0, r] = new_v
            turn[r] = new_v.astype(BF16)

    for d, copy in sent:
        pl.when(exists(d))(copy.wait_send)


def hand_over(*refs):
    count = (len(refs) - 2) // 3
    sources, results, held = (refs[n * count : (n + 1) * count] for n in range(3))
    in_sem, out_sem = refs[-2:]
    into = [pltpu.make_async_copy(sources[n], held[n], in_sem.at[n]) for n in range(count)]
    out = [pltpu.make_async_copy(held[n], results[n], out_sem.at[n]) for n in range(count)]
    for copy in into:
        copy.start()
    for n in range(count):
        into[n].wait()
        out[n].start()
    for copy in out:
        copy.wait()


def passed_on(arrays):
    any_spec = pl.BlockSpec(memory_space=pl.ANY)
    return pl.pallas_call(
        hand_over,
        out_shape=tuple(jax.ShapeDtypeStruct(a.shape, a.dtype) for a in arrays),
        in_specs=[any_spec] * len(arrays),
        out_specs=(any_spec,) * len(arrays),
        scratch_shapes=[pltpu.VMEM(a.shape, a.dtype) for a in arrays]
        + [pltpu.SemaphoreType.DMA((len(arrays),))] * 2,
        compiler_params=pltpu.CompilerParams(vmem_limit_bytes=62 << 20),
    )(*arrays)


def solution(mesh):
    nf, ng = mesh.shape["facet"], mesh.shape["grp"]

    def per_device(image, dual_wave, thresholds, taps, seen, dual_data, radius, blocks, row_ids, col_ids):
        taps = jnp.transpose(taps, (2, 1, 0))
        C, R, L = image.shape
        TAPS, _, NB = taps.shape
        KB, PIX, VB = blocks.shape[2:]
        RB = seen.shape[2]
        T1 = L // TS
        sizes = (nf, ng, NB, C, R, L, KB, RB, PIX, VB, TAPS, 3 * T1)
        vmem = pl.BlockSpec(memory_space=pltpu.VMEM)
        smem = pl.BlockSpec(memory_space=pltpu.SMEM)
        hbm = pl.BlockSpec(memory_space=pltpu.HBM)
        V = pltpu.VMEM
        messages = ITERS * 4 * 8
        results = pl.pallas_call(
            functools.partial(kernel, sizes),
            out_shape=(
                jax.ShapeDtypeStruct(image.shape, F32),
                jax.ShapeDtypeStruct(dual_data.shape, F32),
                jax.ShapeDtypeStruct(dual_wave.shape, BF16),
            ),
            in_specs=[hbm, hbm, hbm, smem, hbm, hbm, smem, hbm, smem, smem],
            out_specs=(vmem, vmem, vmem),
            scratch_shapes=[
                V(image.shape, F32),
                V(dual_wave.shape, BF16),
                V(blocks.shape, BF16),
                V(thresholds.shape, F32),
                V(seen.shape, F32),
                V(dual_data.shape, F32),
                V((NB, 2 * L, L), BF16),
                V((NB, 2 * L, 2 * L), BF16),
                V((NB * R, 3 * R), BF16),
                V((4 * R, NB * R), BF16),
                V((NB * R, C * L + L), BF16),
                V((NB, C, R, 2 * L), BF16),
                V((ITERS, 3, R, C * L), BF16),
                V((8, 128), BF16),
                V((ITERS, 3 * T1, C, PIX), BF16),
                V((ITERS, 2, 3, R, L), BF16),
                V((ITERS, R, L), BF16),
                V((ITERS, R, C * L), BF16),
                V((ITERS, 2, R, C * L), BF16),
                V((ITERS, 2, R, L), BF16),
                V((ITERS, 2, 3, R, L), BF16),
                V((ITERS, 2, T1, C, PIX), BF16),
                V((ITERS, 2, T1, C, PIX), BF16),
                V((KB + 1, C, max(PIX, VB)), F32),
                V(dual_wave.shape, BF16),
                V(image.shape, F32),
                V((R, C * L), F32),
                V((RB, C, VB), BF16),
                pltpu.SMEM((4, max(KB, 3 * T1)), jnp.int32),
                pltpu.SemaphoreType.DMA((6,)),
                pltpu.SemaphoreType.DMA((messages,)),
                pltpu.SemaphoreType.DMA((messages,)),
            ],
            compiler_params=pltpu.CompilerParams(collective_id=0, has_side_effects=True, vmem_limit_bytes=60 << 20),
        )(image, dual_wave, thresholds, taps, seen, dual_data, radius, blocks, row_ids, col_ids)
        return passed_on(results)

    dev = P("facet", "grp")
    rows = P(None, "facet", "grp")
    wave = P(None, None, "facet", "grp")
    return jax.shard_map(
        per_device,
        mesh=mesh,
        in_specs=(rows, wave, rows, P(), dev, dev, dev, dev, dev, dev),
        out_specs=(rows, dev, wave),
        check_vma=False,
    )
```
